32 devices in a mesh: gx: 2 (over x), gy: 4 (over z), gz: 4 (over y, core).
Axes of the slice: x: 2, y: 2, z: 4, core: 2. Of those that a mesh axis runs over, the one named last changes fastest.
Arguments:
- pressure_zero: float32 [32, 64, 1024], P('gx', 'gy', 'gz'), may hold values from -1.2 to 1.2
- pressure_one: float32 [32, 64, 1024], P('gx', 'gy', 'gz'), may hold values from -1.2 to 1.2
- adjoint_upper: float32 [32, 64, 1024], P('gx', 'gy', 'gz'), may hold values from -6 to 6
- adjoint_top: float32 [32, 64, 1024], P('gx', 'gy', 'gz'), may hold values from -6 to 6
- courant_factor: float32 [32, 64, 1024], P('gx', 'gy', 'gz'), may hold values from 0.08 to 0.19
- residual: float32 [4, 1024], P(None, 'gz'), may hold values from -6 to 6
- receiver_cell: int32 [3, 1024], replicated, may hold values from 4 to 1019, as said below
- tap_offset: int32 [3, 16, 1024], replicated, may hold values from -4 to 4
- tap_weight: float32 [16, 1024], replicated, may hold values from -3 to 3
- trace_receiver: int32 [1024], replicated, may hold values from 0 to 1023, each once
Outputs:
- gradient: float32 [32, 64, 1024], P('gx', 'gy', 'gz')
- adjoint_one: float32 [32, 64, 1024], P('gx', 'gy', 'gz')
- adjoint_zero: float32 [32, 64, 1024], P('gx', 'gy', 'gz')
The draws below stay inside these ranges and needn't reach their ends.
Inputs may be any that keep to these rules, and one draw needn't show every extreme that they name: `receiver_cell`: coordinate 0 of a receiver cell lies in 4 to 27, coordinate 1 in 4 to 59, coordinate 2 in 4 to 1019.
All inputs are finite; a program needn't handle non-finite values.
Results may differ from the reference program's by a relative error of at most 0.00002.
Values sent between devices are 32-bit elements; how exact they have to be, the bound alone decides.
A program may use at most 128 MiB of HBM per device.

```python
import math
import jax
import jax.numpy as jnp

STEPS = 4
TAPS = 16
MICS = 1024
NX = 32
NY = 64
NZ = 1024


def draw_receiver_cell(key, part):
    key_centre, key_pick, key_spread = jax.random.split(key, 3)
    limits = jnp.array([NX, NY, NZ], dtype=jnp.int32)[:, None]
    centres = jax.random.randint(key_centre, (3, 8), 0, 1 << 20) % (limits - 8) + 4
    choose = jax.random.randint(key_pick, (MICS,), 0, 8)
    spread = jax.random.randint(key_spread, (3, MICS), -24, 25)
    picked = jnp.take(centres, choose, axis=1) + spread
    placed = jnp.clip(picked, 4, limits - 5)
    placed = placed.at[:, 0].set(limits[:, 0] - 5).at[:, 1].set(4)
    return placed.astype(jnp.int32)


def set_ends(result, rng, smallest, top_value):
    longest = result.shape.index(max(result.shape))
    spots = []
    for shift in (0, 1):
        where = [jax.random.randint(jax.random.fold_in(rng, axis), (), 0, length) for axis, length in enumerate(result.shape)]
        where[longest] = (where[longest] + shift) % result.shape[longest]
        spots.append(tuple(where))
    return result.at[spots[0]].set(smallest).at[spots[1]].set(top_value)


def block_scale(own_key, extent, shards, low, top_value):
    gain, own = 1.0, jax.random.fold_in(own_key, 6)
    for axis_at, parts in shards:
        draws = jnp.exp(jax.random.uniform(jax.random.fold_in(own, axis_at), (parts,), jnp.float32, low / len(shards), top_value / len(shards)))
        gain = gain * jnp.repeat(draws, extent[axis_at] // parts).reshape([-1 if axis == axis_at else 1 for axis in range(len(extent))])
    return gain


def normal_values(stream_key, extent, width, most, cuts=(), kind=jnp.bfloat16):
    loudness = block_scale(stream_key, extent, cuts, -0.22, 0.18) if cuts else 1.0
    entries = jax.random.normal(stream_key, extent, jnp.float32) * width * loudness
    return jnp.minimum(jnp.maximum(entries, -most), most).astype(kind)


def setup_inputs(seed: int = 0) -> dict:
    key_of = jax.random.split(jax.random.key(seed), 11)
    return {
        "pressure_zero": normal_values(key_of[0], (NX, NY, NZ), 0.2, 1.2, ((0, 2), (1, 4), (2, 4)), jnp.float32),
        "pressure_one": normal_values(key_of[1], (NX, NY, NZ), 0.2, 1.2, ((0, 2), (1, 4), (2, 4)), jnp.float32),
        "adjoint_upper": normal_values(key_of[2], (NX, NY, NZ), 1.0, 6.0, ((0, 2), (1, 4), (2, 4)), jnp.float32),
        "adjoint_top": normal_values(key_of[3], (NX, NY, NZ), 1.0, 6.0, ((0, 2), (1, 4), (2, 4)), jnp.float32),
        "courant_factor": jnp.clip(jnp.exp(math.log(0.19) - 0.86499745 * jax.random.uniform(key_of[4], (NX, NY, NZ), jnp.float32) ** block_scale(key_of[4], (NX, NY, NZ), ((0, 2), (1, 4), (2, 4)), -0.2, 0.2)), 0.08, 0.19),
        "residual": normal_values(key_of[5], (STEPS, MICS), 1.0, 6.0, ((1, 4),), jnp.float32),
        "receiver_cell": draw_receiver_cell(jax.random.fold_in(key_of[10], 71), 0),
        "tap_offset": set_ends(jax.random.randint(key_of[7], (3, TAPS, MICS), -4, 5), jax.random.fold_in(key_of[7], 1), -4, 4).astype(jnp.int32),
        "tap_weight": normal_values(key_of[8], (TAPS, MICS), 0.5, 3.0, (), jnp.float32),
        "trace_receiver": jax.random.permutation(key_of[9], MICS).astype(jnp.int32),
    }


STENCIL_WEIGHTS = (-205.0 / 72.0, 8.0 / 5.0, -1.0 / 5.0, 8.0 / 315.0, -1.0 / 560.0)


def laplace(grid_field):
    size_x, size_y, size_z = grid_field.shape[-3:]
    centre = grid_field[..., 4:size_x - 4, 4:size_y - 4, 4:size_z - 4]
    summed = (3.0 * STENCIL_WEIGHTS[0]) * centre
    for reach in range(1, 5):
        summed = summed + STENCIL_WEIGHTS[reach] * (
            grid_field[..., 4 + reach:size_x - 4 + reach, 4:size_y - 4, 4:size_z - 4]
            + grid_field[..., 4 - reach:size_x - 4 - reach, 4:size_y - 4, 4:size_z - 4]
            + grid_field[..., 4:size_x - 4, 4 + reach:size_y - 4 + reach, 4:size_z - 4]
            + grid_field[..., 4:size_x - 4, 4 - reach:size_y - 4 - reach, 4:size_z - 4]
            + grid_field[..., 4:size_x - 4, 4:size_y - 4, 4 + reach:size_z - 4 + reach]
            + grid_field[..., 4:size_x - 4, 4:size_y - 4, 4 - reach:size_z - 4 - reach])
    return summed


def laplace_full(grid_field):
    return laplace(jnp.pad(grid_field, 4))


def reference(pressure_zero, pressure_one, adjoint_upper, adjoint_top, courant_factor, residual, receiver_cell, tap_offset, tap_weight, trace_receiver):
    step_count = residual.shape[0]
    earlier, current = pressure_zero, pressure_one
    laplacians = []
    for level in range(step_count):
        curvature = laplace_full(current)
        laplacians.append(curvature)
        if level + 1 < step_count:
            earlier, current = current, 2.0 * current - earlier + courant_factor * curvature
    mic_cells = jnp.take(receiver_cell, trace_receiver, axis=1)
    tap_cells = jnp.take(tap_offset, trace_receiver, axis=2)
    weights = jnp.take(tap_weight, trace_receiver, axis=1)
    position = mic_cells[:, None, :] + tap_cells
    flat_index = ((position[0] * NY + position[1]) * NZ + position[2]).reshape(-1).astype(jnp.int32)
    amounts = weights[None, :, :] * residual[:, None, :]
    upper_level, level_now = adjoint_upper, adjoint_top
    gradient = jnp.zeros_like(adjoint_top)
    for level in range(step_count, 0, -1):
        gradient = gradient + level_now * laplacians[level - 1]
        lowered = 2.0 * level_now - upper_level + laplace_full(courant_factor * level_now)
        lowered = lowered.reshape(-1).at[flat_index].add(amounts[level - 1].reshape(-1)).reshape(level_now.shape)
        upper_level, level_now = level_now, lowered
    return gradient, upper_level, level_now
```

```python
import functools

import jax
import jax.numpy as jnp
from jax import lax
from jax.experimental import pallas as pl
from jax.experimental.pallas import tpu as pltpu
from jax.sharding import PartitionSpec as P

C = (-205.0 / 72.0, 8.0 / 5.0, -1.0 / 5.0, 8.0 / 315.0, -1.0 / 560.0)
AXES = ("gx", "gy", "gz")
MESH = pl.DeviceIdType.MESH


def split3(v):
    hi = v.astype(jnp.bfloat16)
    rest = v - hi.astype(jnp.float32)
    mid = rest.astype(jnp.bfloat16)
    lo = (rest - mid.astype(jnp.float32)).astype(jnp.bfloat16)
    return [hi, mid, lo]


def nt(a, b):
    return lax.dot_general(a, b, (((1,), (1,)), ((), ())), preferred_element_type=jnp.float32)


def source_kernel(block, res_ref, cell_ref, off_ref, w_ref, tr_ref, out_ref, table, info):
    bx, by, bz = block
    starts = [lax.axis_index(a) * n for a, n in zip(AXES, block)]
    taps, mics = w_ref.shape
    steps = res_ref.shape[0]
    rel = [cell_ref[d : d + 1, :] - starts[d] for d in range(3)]
    near = functools.reduce(
        jnp.logical_and, [(rel[d] >= -4) & (rel[d] < block[d] + 4) for d in range(3)]
    )
    at = [rel[d] + off_ref[d] for d in range(3)]
    inside = functools.reduce(
        jnp.logical_and, [(at[d] >= 0) & (at[d] < block[d]) for d in range(3)]
    )
    row = jnp.where(inside, at[0] * by + at[1], -1)
    col = jnp.where(inside, at[2], -1)
    table[0:taps, :] = row.astype(jnp.float32).astype(jnp.bfloat16)
    table[taps : 2 * taps, :] = col.astype(jnp.float32).astype(jnp.bfloat16)
    for i, part in enumerate(split3(w_ref[...])):
        table[(2 + i) * taps : (3 + i) * taps, :] = part
    near_f = jnp.where(near, 1.0, 0.0)
    lanes = 128
    blocks = mics // lanes
    tri = (
        lax.broadcasted_iota(jnp.int32, (lanes, lanes), 0)
        < lax.broadcasted_iota(jnp.int32, (lanes, lanes), 1)
    )
    tri = jnp.where(tri, 1.0, 0.0).astype(jnp.bfloat16)
    base = jnp.float32(0.0)
    for i in range(blocks):
        part = near_f[:, i * lanes : (i + 1) * lanes]
        before = jnp.dot(
            jnp.broadcast_to(part, (8, lanes)).astype(jnp.bfloat16),
            tri,
            preferred_element_type=jnp.float32,
        )[0:1]
        slot = jnp.where(part > 0.5, before + base, -1.0)
        info[0:1, i * lanes : (i + 1) * lanes] = slot
        base = base + jnp.sum(part)
    count = base.astype(jnp.int32)
    out_ref[...] = jnp.zeros_like(out_ref)

    def chunk(j, carry):
        slots = (lax.broadcasted_iota(jnp.int32, (lanes, mics), 0) + j * lanes).astype(jnp.float32)
        sel = jnp.where(slots == info[0:1, :], 1.0, 0.0)
        mic_id = lax.broadcasted_iota(jnp.int32, (1, mics), 1).astype(jnp.float32)
        mic = jnp.sum(sel * (mic_id + 1.0), axis=1, keepdims=True) - 1.0
        sel_r = jnp.where(tr_ref[...].astype(jnp.float32) == mic, 1.0, 0.0).astype(jnp.bfloat16)
        tab = nt(table[...], sel.astype(jnp.bfloat16))
        rows = tab[0:taps]
        cols = tab[taps : 2 * taps]
        weights = tab[2 * taps : 3 * taps] + tab[3 * taps : 4 * taps] + tab[4 * taps : 5 * taps]
        res = sum(nt(part, sel_r) for part in split3(res_ref[...]))
        iota_row = lax.broadcasted_iota(jnp.int32, (bx * by, lanes), 0).astype(jnp.float32)
        iota_col = lax.broadcasted_iota(jnp.int32, (bz, lanes), 0).astype(jnp.float32)
        group = 4
        for t0 in range(0, taps, group):
            left, right = [[] for _ in range(steps)], []
            for t in range(t0, t0 + group):
                row_hot = iota_row == rows[t : t + 1]
                col_hot = jnp.where(iota_col == cols[t : t + 1], 1.0, 0.0).astype(jnp.bfloat16)
                right += [col_hot, col_hot]
                for n in range(steps):
                    amount = weights[t : t + 1] * res[n : n + 1]
                    hi = amount.astype(jnp.bfloat16).astype(jnp.float32)
                    lo = amount - hi
                    left[n].append(jnp.where(row_hot, hi, 0.0).astype(jnp.bfloat16))
                    left[n].append(jnp.where(row_hot, lo, 0.0).astype(jnp.bfloat16))
            right = jnp.concatenate(right, axis=1)
            for n in range(steps):
                out_ref[n] += nt(jnp.concatenate(left[n], axis=1), right)
        return carry

    lax.fori_loop(0, (count + lanes - 1) // lanes, chunk, 0)


def build_sources(block, residual, receiver_cell, tap_offset, tap_weight, trace_receiver):
    steps = residual.shape[0]
    taps, mics = tap_weight.shape
    return pl.pallas_call(
        functools.partial(source_kernel, block),
        out_shape=jax.ShapeDtypeStruct((steps, block[0] * block[1], block[2]), jnp.float32),
        in_specs=[pl.BlockSpec(memory_space=pltpu.VMEM)] * 5,
        out_specs=pl.BlockSpec(memory_space=pltpu.VMEM),
        scratch_shapes=[
            pltpu.VMEM((5 * taps, mics), jnp.bfloat16),
            pltpu.VMEM((8, mics), jnp.float32),
        ],
        compiler_params=pltpu.CompilerParams(vmem_limit_bytes=40 * 2**20),
        name="sources",
    )(residual, receiver_cell, tap_offset, tap_weight, trace_receiver.reshape(1, mics))


def wave_kernel(
    sizes, p0, p1, q5, q4, cf, src, grad, one, zero,
    fp, fq, lap, lq, qb, xl, yl, zl, ys, send_sem, recv_sem,
):
    steps = src.shape[0]
    nx, ny, nz = p0.shape
    me = [lax.axis_index(a) for a in AXES]
    has = []
    for d in range(3):
        has += [me[d] > 0, me[d] < sizes[d] - 1]
    to = []
    for d in range(3):
        to += [{AXES[d]: jnp.maximum(me[d] - 1, 0)}, {AXES[d]: jnp.minimum(me[d] + 1, sizes[d] - 1)}]

    barrier = pltpu.get_barrier_semaphore()
    for f in range(6):
        @pl.when(has[f])
        def _(f=f):
            pl.semaphore_signal(barrier, inc=1, device_id=to[f], device_id_type=MESH)
    pl.semaphore_wait(barrier, sum(h.astype(jnp.int32) for h in has))

    fields = (fp, fq)
    mid = (pl.ds(4, nx), pl.ds(8, ny))
    sub = lax.broadcasted_iota(jnp.int32, (8, nz), 0)
    lane = lax.broadcasted_iota(jnp.int32, (ny, 128), 1)

    def copies(ch, r):
        f_ref = fields[ch].at[r]
        srcs = [
            f_ref.at[pl.ds(4, 4), pl.ds(8, ny)],
            f_ref.at[pl.ds(nx, 4), pl.ds(8, ny)],
            ys.at[ch, r, 0],
            ys.at[ch, r, 1],
            f_ref.at[pl.ds(4, nx), pl.ds(8, ny), pl.ds(0, 128)],
            f_ref.at[pl.ds(4, nx), pl.ds(8, ny), pl.ds(nz - 128, 128)],
        ]
        lands = (xl, xl, yl, yl, zl, zl)
        out = []
        for f in range(6):
            out.append(
                pltpu.make_async_remote_copy(
                    src_ref=srcs[f],
                    dst_ref=lands[f].at[ch, r, 1 - f % 2],
                    send_sem=send_sem.at[ch, r, f],
                    recv_sem=recv_sem.at[ch, r, f ^ 1],
                    device_id=to[f],
                    device_id_type=MESH,
                )
            )
        return out

    def send(ch, r):
        f_ref = fields[ch]
        moves = copies(ch, r)
        for f in (0, 1, 4, 5):
            @pl.when(has[f])
            def _(f=f):
                moves[f].start()

        def pack(i, carry):
            a, b = f_ref[r, 4 + i, pl.ds(8, 8)], f_ref[r, 4 + i + nx // 2, pl.ds(8, 8)]
            ys[ch, r, 0, i] = jnp.where(sub < 4, a, pltpu.roll(b, 4, 0))
            a, b = f_ref[r, 4 + i, pl.ds(ny, 8)], f_ref[r, 4 + i + nx // 2, pl.ds(ny, 8)]
            ys[ch, r, 1, i] = jnp.where(sub >= 4, a, pltpu.roll(b, 4, 0))
            return carry

        lax.fori_loop(0, nx // 2, pack, 0)
        for f in (2, 3):
            @pl.when(has[f])
            def _(f=f):
                moves[f].start()

    def land(ch, r, d):
        for f in (2 * d, 2 * d + 1):
            @pl.when(has[f])
            def _(f=f):
                dst = (xl, yl, zl)[d].at[ch, r, f % 2]
                pltpu.make_async_remote_copy(
                    src_ref=dst, dst_ref=dst,
                    send_sem=send_sem.at[ch, r, f], recv_sem=recv_sem.at[ch, r, f],
                    device_id=to[f], device_id_type=MESH,
                ).wait_recv()

    def local(ch, r, out):
        f_ref = fields[ch]

        def plane(i, carry):
            c = f_ref[r, 4 + i, pl.ds(8, ny)]
            acc = 3.0 * C[0] * c
            for k in range(1, 5):
                acc = acc + C[k] * (
                    (f_ref[r, 4 + i + k, pl.ds(8, ny)] + f_ref[r, 4 + i - k, pl.ds(8, ny)])
                    + (f_ref[r, 4 + i, pl.ds(8 + k, ny)] + f_ref[r, 4 + i, pl.ds(8 - k, ny)])
                    + (pltpu.roll(c, k, 1) + pltpu.roll(c, nz - k, 1))
                )
            out[i] = acc
            return carry

        lax.fori_loop(0, nx, plane, 0)

    def finish(ch, r, out, update):
        f_ref = fields[ch]
        land(ch, r, 0)
        for j in range(4):
            out[j] += sum(C[k] * xl[ch, r, 0, 4 + j - k] for k in range(j + 1, 5))
            out[nx - 4 + j] += sum(C[k] * xl[ch, r, 1, j + k - 4] for k in range(4 - j, 5))
        land(ch, r, 1)
        land(ch, r, 2)

        def plane(i, carry):
            lo, hi = yl[ch, r, 0, i], yl[ch, r, 1, i]
            for half in range(2):
                x = i + half * (nx // 2)
                if half:
                    lo, hi = pltpu.roll(lo, 4, 0), pltpu.roll(hi, 4, 0)
                fix_lo = sum(
                    C[k] * jnp.where(sub < k, pltpu.roll(lo, k, 0), 0.0) for k in range(1, 5)
                )
                fix_hi = sum(
                    C[k] * jnp.where(sub >= 8 - k, pltpu.roll(hi, 8 - k, 0), 0.0)
                    for k in range(1, 5)
                )
                d_lo = zl[ch, r, 0, x] - f_ref[r, 4 + x, pl.ds(8, ny), pl.ds(nz - 128, 128)]
                d_hi = zl[ch, r, 1, x] - f_ref[r, 4 + x, pl.ds(8, ny), pl.ds(0, 128)]
                z_lo = sum(
                    C[k] * jnp.where(lane < k, pltpu.roll(d_lo, k, 1), 0.0) for k in range(1, 5)
                )
                z_hi = sum(
                    C[k] * jnp.where(lane >= 128 - k, pltpu.roll(d_hi, 128 - k, 1), 0.0)
                    for k in range(1, 5)
                )
                parts = [z_lo] + [jnp.zeros_like(z_lo)] * (nz // 128 - 2) + [z_hi]
                full = out[x] + jnp.concatenate(parts, axis=1)
                rows = [fix_lo] + [jnp.zeros_like(fix_lo)] * (ny // 8 - 2) + [fix_hi]
                full = full + jnp.concatenate(rows, axis=0)
                out[x] = full
                update(x, full)
            return carry

        lax.fori_loop(0, nx // 2, plane, 0)

    fp[0, mid[0], mid[1]] = p1[...]
    send(0, 0)
    fq[0, mid[0], mid[1]] = cf[...] * q4[...]
    send(1, 0)
    for f_ref in fields:
        for r in range(steps):
            f_ref[r, pl.ds(0, 4), pl.ds(8, ny)] = jnp.zeros((4, ny, nz), jnp.float32)
            f_ref[r, pl.ds(4 + nx, 4), pl.ds(8, ny)] = jnp.zeros((4, ny, nz), jnp.float32)
            f_ref[r, mid[0], pl.ds(0, 8)] = jnp.zeros((nx, 8, nz), jnp.float32)
            f_ref[r, mid[0], pl.ds(8 + ny, 8)] = jnp.zeros((nx, 8, nz), jnp.float32)
    for f in range(6):
        @pl.when(jnp.logical_not(has[f]))
        def _(f=f):
            for ch in range(2):
                for r in range(steps):
                    dst = (xl, yl, zl)[f // 2].at[ch, r, f % 2]
                    dst[...] = jnp.zeros(dst.shape, jnp.float32)

    local(0, 0, lap.at[0])
    local(1, 0, lq)
    for r in range(steps):
        def up_p(x, full, r=r):
            if r + 1 < steps:
                old = p0[x] if r == 0 else fp[r - 1, 4 + x, pl.ds(8, ny)]
                now = fp[r, 4 + x, pl.ds(8, ny)]
                fp[r + 1, 4 + x, pl.ds(8, ny)] = 2.0 * now - old + cf[x] * full

        finish(0, r, lap.at[r], up_p)
        if r + 1 < steps:
            send(0, r + 1)
            local(0, r + 1, lap.at[r + 1])

        def up_q(x, full, r=r):
            now = q4[x] if r == 0 else qb[r - 1, x]
            old = q5[x] if r == 0 else (q4[x] if r == 1 else qb[r - 2, x])
            new = 2.0 * now - old + full + src[steps - 1 - r, pl.ds(pl.multiple_of(x * ny, ny), ny)]
            if r + 1 < steps:
                qb[r, x] = new
                fq[r + 1, 4 + x, pl.ds(8, ny)] = cf[x] * new
            else:
                zero[x] = new
                one[x] = now
                total = q4[x] * lap[steps - 1, x]
                for n in range(1, steps):
                    total = total + qb[n - 1, x] * lap[steps - 1 - n, x]
                grad[x] = total

        finish(1, r, lq, up_q)
        if r + 1 < steps:
            send(1, r + 1)
            local(1, r + 1, lq)

    for ch in range(2):
        for r in range(steps):
            moves = copies(ch, r)
            for f in range(6):
                @pl.when(has[f])
                def _(f=f):
                    moves[f].wait_send()


def wave(sizes, p0, p1, q5, q4, cf, src):
    nx, ny, nz = p0.shape
    steps = src.shape[0]
    f32 = jnp.float32
    return pl.pallas_call(
        functools.partial(wave_kernel, sizes),
        out_shape=[jax.ShapeDtypeStruct(p0.shape, f32)] * 3,
        in_specs=[pl.BlockSpec(memory_space=pltpu.VMEM)] * 6,
        out_specs=[pl.BlockSpec(memory_space=pltpu.VMEM)] * 3,
        scratch_shapes=[
            pltpu.VMEM((steps, nx + 8, ny + 16, nz), f32),
            pltpu.VMEM((steps, nx + 8, ny + 16, nz), f32),
            pltpu.VMEM((steps, nx, ny, nz), f32),
            pltpu.VMEM((nx, ny, nz), f32),
            pltpu.VMEM((steps, nx, ny, nz), f32),
            pltpu.VMEM((2, steps, 2, 4, ny, nz), f32),
            pltpu.VMEM((2, steps, 2, nx // 2, 8, nz), f32),
            pltpu.VMEM((2, steps, 2, nx, ny, 128), f32),
            pltpu.VMEM((2, steps, 2, nx // 2, 8, nz), f32),
            pltpu.SemaphoreType.DMA((2, steps, 6)),
            pltpu.SemaphoreType.DMA((2, steps, 6)),
        ],
        compiler_params=pltpu.CompilerParams(
            collective_id=0, has_side_effects=True, vmem_limit_bytes=48 * 2**20
        ),
        name="wave",
    )(p0, p1, q5, q4, cf, src)


def shards(sizes, p0, p1, q5, q4, cf, residual, receiver_cell, tap_offset, tap_weight, trace_receiver):
    gathered = lax.all_gather(residual, "gz", axis=1, tiled=True)
    src = build_sources(p0.shape, gathered, receiver_cell, tap_offset, tap_weight, trace_receiver)
    return tuple(wave(sizes, p0, p1, q5, q4, cf, src))


def solution(mesh):
    field = P(*AXES)
    return jax.shard_map(
        functools.partial(shards, tuple(mesh.shape[a] for a in AXES)),
        mesh=mesh,
        in_specs=(field,) * 5 + (P(None, "gz"), P(), P(), P(), P()),
        out_specs=(field,) * 3,
        check_vma=False,
    )
```

```python
import functools

import jax
import jax.numpy as jnp
import ml_dtypes
import numpy as np
from jax import lax
from jax.experimental import pallas as pl
from jax.experimental.pallas import tpu as pltpu
from jax.sharding import PartitionSpec as P

C = (-205.0 / 72.0, 8.0 / 5.0, -1.0 / 5.0, 8.0 / 315.0, -1.0 / 560.0)
AXES = ("gx", "gy", "gz")
MESH = pl.DeviceIdType.MESH


def split3(v):
    hi = v.astype(jnp.bfloat16)
    rest = v - hi.astype(jnp.float32)
    mid = rest.astype(jnp.bfloat16)
    lo = (rest - mid.astype(jnp.float32)).astype(jnp.bfloat16)
    return [hi, mid, lo]


def nt(a, b):
    return lax.dot_general(a, b, (((1,), (1,)), ((), ())), preferred_element_type=jnp.float32)


def source_kernel(block, res_ref, cell_ref, off_ref, w_ref, tr_ref, out_ref, table, info):
    bx, by, bz = block
    starts = [lax.axis_index(a) * n for a, n in zip(AXES, block)]
    taps, mics = w_ref.shape
    steps = res_ref.shape[0]
    rel = [cell_ref[d : d + 1, :] - starts[d] for d in range(3)]
    near = functools.reduce(
        jnp.logical_and, [(rel[d] >= -4) & (rel[d] < block[d] + 4) for d in range(3)]
    )
    at = [rel[d] + off_ref[d] for d in range(3)]
    inside = functools.reduce(
        jnp.logical_and, [(at[d] >= 0) & (at[d] < block[d]) for d in range(3)]
    )
    row = jnp.where(inside, at[0] * by + at[1], -1)
    col = jnp.where(inside, at[2], -1)
    table[0:taps, :] = row.astype(jnp.float32).astype(jnp.bfloat16)
    table[taps : 2 * taps, :] = col.astype(jnp.float32).astype(jnp.bfloat16)
    for i, part in enumerate(split3(w_ref[...])):
        table[(2 + i) * taps : (3 + i) * taps, :] = part
    near_f = jnp.where(near, 1.0, 0.0)
    lanes = 128
    blocks = mics // lanes
    tri = (
        lax.broadcasted_iota(jnp.int32, (lanes, lanes), 0)
        < lax.broadcasted_iota(jnp.int32, (lanes, lanes), 1)
    )
    tri = jnp.where(tri, 1.0, 0.0).astype(jnp.bfloat16)
    base = jnp.float32(0.0)
    for i in range(blocks):
        part = near_f[:, i * lanes : (i + 1) * lanes]
        before = jnp.dot(
            jnp.broadcast_to(part, (8, lanes)).astype(jnp.bfloat16),
            tri,
            preferred_element_type=jnp.float32,
        )[0:1]
        slot = jnp.where(part > 0.5, before + base, -1.0)
        info[0:1, i * lanes : (i + 1) * lanes] = slot
        base = base + jnp.sum(part)
    count = base.astype(jnp.int32)
    out_ref[...] = jnp.zeros_like(out_ref)

    def chunk(j, carry):
        slots = (lax.broadcasted_iota(jnp.int32, (lanes, mics), 0) + j * lanes).astype(jnp.float32)
        sel = jnp.where(slots == info[0:1, :], 1.0, 0.0)
        mic_id = lax.broadcasted_iota(jnp.int32, (1, mics), 1).astype(jnp.float32)
        mic = jnp.sum(sel * (mic_id + 1.0), axis=1, keepdims=True) - 1.0
        sel_r = jnp.where(tr_ref[...].astype(jnp.float32) == mic, 1.0, 0.0).astype(jnp.bfloat16)
        tab = nt(table[...], sel.astype(jnp.bfloat16))
        rows = tab[0:taps]
        cols = tab[taps : 2 * taps]
        weights = tab[2 * taps : 3 * taps] + tab[3 * taps : 4 * taps] + tab[4 * taps : 5 * taps]
        res = sum(nt(part, sel_r) for part in split3(res_ref[...]))
        iota_row = lax.broadcasted_iota(jnp.int32, (bx * by, lanes), 0).astype(jnp.float32)
        iota_col = lax.broadcasted_iota(jnp.int32, (bz, lanes), 0).astype(jnp.float32)
        group = 4
        for t0 in range(0, taps, group):
            left, right = [[] for _ in range(steps)], []
            for t in range(t0, t0 + group):
                row_hot = iota_row == rows[t : t + 1]
                col_hot = jnp.where(iota_col == cols[t : t + 1], 1.0, 0.0).astype(jnp.bfloat16)
                right += [col_hot, col_hot]
                for n in range(steps):
                    amount = weights[t : t + 1] * res[n : n + 1]
                    hi = amount.astype(jnp.bfloat16).astype(jnp.float32)
                    lo = amount - hi
                    left[n].append(jnp.where(row_hot, hi, 0.0).astype(jnp.bfloat16))
                    left[n].append(jnp.where(row_hot, lo, 0.0).astype(jnp.bfloat16))
            right = jnp.concatenate(right, axis=1)
            for n in range(steps):
                out_ref[n] += nt(jnp.concatenate(left[n], axis=1), right)
        return carry

    lax.fori_loop(0, (count + lanes - 1) // lanes, chunk, 0)


def build_sources(block, residual, receiver_cell, tap_offset, tap_weight, trace_receiver):
    steps = residual.shape[0]
    taps, mics = tap_weight.shape
    return pl.pallas_call(
        functools.partial(source_kernel, block),
        out_shape=jax.ShapeDtypeStruct((steps, block[0] * block[1], block[2]), jnp.float32),
        in_specs=[pl.BlockSpec(memory_space=pltpu.VMEM)] * 5,
        out_specs=pl.BlockSpec(memory_space=pltpu.VMEM),
        scratch_shapes=[
            pltpu.VMEM((5 * taps, mics), jnp.bfloat16),
            pltpu.VMEM((8, mics), jnp.float32),
        ],
        compiler_params=pltpu.CompilerParams(vmem_limit_bytes=40 * 2**20),
        name="sources",
    )(residual, receiver_cell, tap_offset, tap_weight, trace_receiver.reshape(1, mics))


def matrices(nx, ny, nz):
    weight = {k: round(5040 * C[abs(k)]) if k else 0 for k in range(-4, 5)}
    at = np.vectorize(lambda k: weight.get(int(k), 0))
    x, y = np.divmod(np.arange(nx * ny), ny)
    dx, dy = x[:, None] - x[None, :], y[:, None] - y[None, :]
    inner = at(dx) * (dy == 0) + at(dy) * (dx == 0)
    fx, fy = np.divmod(np.arange(4 * ny), ny)
    tile, sub = np.divmod(np.arange(4 * nx), 8)
    lo_x = tile + np.where(sub >= 4, 0, nx // 2)
    hi_x = tile + np.where(sub < 4, 0, nx // 2)
    face_x = np.concatenate([fx - 4, fx + nx, lo_x, hi_x])
    face_y = np.concatenate([fy, fy, sub % 4 - 4, sub % 4 + ny])
    dx, dy = x[:, None] - face_x[None, :], y[:, None] - face_y[None, :]
    faces = at(dx) * (dy == 0) + at(dy) * (dx == 0)
    z = np.arange(nz)
    along = at(z[:, None] - z[None, :])
    end = np.arange(128)
    end = np.where(end < 64, end + nz, end - 128)
    ends = at(end[:, None] - z[None, :])
    return [m.astype(ml_dtypes.bfloat16) for m in (inner, faces, along, ends)]


def nn(a, b):
    return jnp.dot(a, b, preferred_element_type=jnp.float32)


def wave_kernel(
    sizes, ny, p0, p1, q5, q4, cf, src, m_in, m_face, m_z, m_end, grad, one, zero,
    fp, fq, lap, lq, qb, hl, zl, ys, send_sem, recv_sem,
):
    steps = src.shape[0]
    rows, nz = p0.shape
    nx = rows // ny
    faces_rows = (4 * ny, 4 * ny, 4 * nx, 4 * nx)
    me = [lax.axis_index(a) for a in AXES]
    has = []
    for d in range(3):
        has += [me[d] > 0, me[d] < sizes[d] - 1]
    to = []
    for d in range(3):
        to += [{AXES[d]: jnp.maximum(me[d] - 1, 0)}, {AXES[d]: jnp.minimum(me[d] + 1, sizes[d] - 1)}]

    barrier = pltpu.get_barrier_semaphore()
    for f in range(6):
        @pl.when(has[f])
        def _(f=f):
            pl.semaphore_signal(barrier, inc=1, device_id=to[f], device_id_type=MESH)
    pl.semaphore_wait(barrier, sum(h.astype(jnp.int32) for h in has))

    sub = lax.broadcasted_iota(jnp.int32, (8, nz), 0)
    lane = lax.broadcasted_iota(jnp.int32, (rows, 128), 1)

    def field(ch, r):
        if r == 0 and ch == 0:
            return p1
        return (fp, fq)[ch].at[r]

    def landing(ch, r, f):
        if f >= 4:
            return zl.at[ch, r, f - 4]
        return hl.at[ch, r, pl.ds(sum(faces_rows[:f]), faces_rows[f])]

    def copies(ch, r):
        f_ref = field(ch, r)
        srcs = [
            f_ref.at[pl.ds(0, 4 * ny)],
            f_ref.at[pl.ds(rows - 4 * ny, 4 * ny)],
            ys.at[ch, r, 0],
            ys.at[ch, r, 1],
            f_ref.at[pl.ds(0, rows), pl.ds(0, 128)],
            f_ref.at[pl.ds(0, rows), pl.ds(nz - 128, 128)],
        ]
        return [
            pltpu.make_async_remote_copy(
                src_ref=srcs[f],
                dst_ref=landing(ch, r, f ^ 1),
                send_sem=send_sem.at[ch, r, f],
                recv_sem=recv_sem.at[ch, r, f ^ 1],
                device_id=to[f],
                device_id_type=MESH,
            )
            for f in range(6)
        ]

    def send(ch, r):
        f_ref = field(ch, r)
        moves = copies(ch, r)
        for f in (0, 1, 4, 5):
            @pl.when(has[f])
            def _(f=f):
                moves[f].start()
        for i in range(nx // 2):
            lo, far = i * ny, (i + nx // 2) * ny
            a, b = f_ref[lo : lo + 8], f_ref[far : far + 8]
            ys[ch, r, 0, 8 * i : 8 * i + 8] = jnp.where(sub < 4, a, pltpu.roll(b, 4, 0))
            a, b = f_ref[lo + ny - 8 : lo + ny], f_ref[far + ny - 8 : far + ny]
            ys[ch, r, 1, 8 * i : 8 * i + 8] = jnp.where(sub >= 4, a, pltpu.roll(b, 4, 0))
        for f in (2, 3):
            @pl.when(has[f])
            def _(f=f):
                moves[f].start()

    def land(ch, r):
        for f in range(6):
            @pl.when(has[f])
            def _(f=f):
                dst = landing(ch, r, f)
                pltpu.make_async_remote_copy(
                    src_ref=dst, dst_ref=dst,
                    send_sem=send_sem.at[ch, r, f], recv_sem=recv_sem.at[ch, r, f],
                    device_id=to[f], device_id_type=MESH,
                ).wait_recv()

    def local(ch, r, out):
        f = field(ch, r)[...]
        acc = 0.0
        for part in split3(f):
            acc = acc + nn(m_in[...], part) + nn(part, m_z[...])
        out[...] = acc * (1.0 / 5040.0) + (3.0 * C[0]) * f

    def finish(ch, r, out):
        land(ch, r)
        acc = 0.0
        for part in split3(hl[ch, r]):
            acc = acc + nn(m_face[...], part)
        for part in split3(jnp.where(lane < 64, zl[ch, r, 1], zl[ch, r, 0])):
            acc = acc + nn(part, m_end[...])
        return out[...] + acc * (1.0 / 5040.0)

    send(0, 0)
    fq[0] = cf[...] * q4[...]
    send(1, 0)
    for f in range(6):
        @pl.when(jnp.logical_not(has[f]))
        def _(f=f):
            for ch in range(2):
                for r in range(steps):
                    dst = landing(ch, r, f)
                    dst[...] = jnp.zeros(dst.shape, jnp.float32)

    local(0, 0, lap.at[0])
    local(1, 0, lq)
    for r in range(steps):
        full = finish(0, r, lap.at[r])
        lap[r] = full
        if r + 1 < steps:
            old = p0 if r == 0 else field(0, r - 1)
            fp[r + 1] = 2.0 * field(0, r)[...] - old[...] + cf[...] * full
            send(0, r + 1)
            local(0, r + 1, lap.at[r + 1])

        full = finish(1, r, lq)
        now = q4 if r == 0 else qb.at[r - 1]
        old = q5 if r == 0 else (q4 if r == 1 else qb.at[r - 2])
        new = 2.0 * now[...] - old[...] + full + src[steps - 1 - r]
        if r + 1 < steps:
            qb[r] = new
            fq[r + 1] = cf[...] * new
            send(1, r + 1)
            local(1, r + 1, lq)
        else:
            zero[...] = new
            one[...] = now[...]
            total = q4[...] * lap[steps - 1]
            for n in range(1, steps):
                total = total + qb[n - 1] * lap[steps - 1 - n]
            grad[...] = total

    for ch in range(2):
        for r in range(steps):
            moves = copies(ch, r)
            for f in range(6):
                @pl.when(has[f])
                def _(f=f):
                    moves[f].wait_send()


def wave(sizes, p0, p1, q5, q4, cf, src):
    nx, ny, nz = p0.shape
    steps = src.shape[0]
    rows = nx * ny
    f32 = jnp.float32
    flat = [a.reshape(rows, nz) for a in (p0, p1, q5, q4, cf)]
    outs = pl.pallas_call(
        functools.partial(wave_kernel, sizes, ny),
        out_shape=[jax.ShapeDtypeStruct((rows, nz), f32)] * 3,
        in_specs=[pl.BlockSpec(memory_space=pltpu.VMEM)] * 10,
        out_specs=[pl.BlockSpec(memory_space=pltpu.VMEM)] * 3,
        scratch_shapes=[
            pltpu.VMEM((steps, rows, nz), f32),
            pltpu.VMEM((steps, rows, nz), f32),
            pltpu.VMEM((steps, rows, nz), f32),
            pltpu.VMEM((rows, nz), f32),
            pltpu.VMEM((steps, rows, nz), f32),
            pltpu.VMEM((2, steps, 8 * (nx + ny), nz), f32),
            pltpu.VMEM((2, steps, 2, rows, 128), f32),
            pltpu.VMEM((2, steps, 2, 4 * nx, nz), f32),
            pltpu.SemaphoreType.DMA((2, steps, 6)),
            pltpu.SemaphoreType.DMA((2, steps, 6)),
        ],
        compiler_params=pltpu.CompilerParams(
            collective_id=0, has_side_effects=True, vmem_limit_bytes=48 * 2**20
        ),
        name="wave",
    )(*flat, src, *matrices(nx, ny, nz))
    return [o.reshape(nx, ny, nz) for o in outs]


def shards(sizes, p0, p1, q5, q4, cf, residual, receiver_cell, tap_offset, tap_weight, trace_receiver):
    gathered = lax.all_gather(residual, "gz", axis=1, tiled=True)
    src = build_sources(p0.shape, gathered, receiver_cell, tap_offset, tap_weight, trace_receiver)
    return tuple(wave(sizes, p0, p1, q5, q4, cf, src))


def solution(mesh):
    field = P(*AXES)
    return jax.shard_map(
        functools.partial(shards, tuple(mesh.shape[a] for a in AXES)),
        mesh=mesh,
        in_specs=(field,) * 5 + (P(None, "gz"), P(), P(), P(), P()),
        out_specs=(field,) * 3,
        check_vma=False,
    )
```

```python
import functools

import jax
import jax.numpy as jnp
import ml_dtypes
import numpy as np
from jax import lax
from jax.experimental import pallas as pl
from jax.experimental.pallas import tpu as pltpu
from jax.sharding import PartitionSpec as P

C = (-205.0 / 72.0, 8.0 / 5.0, -1.0 / 5.0, 8.0 / 315.0, -1.0 / 560.0)
AXES = ("gx", "gy", "gz")
MESH = pl.DeviceIdType.MESH


def split3(v):
    hi = v.astype(jnp.bfloat16)
    rest = v - hi.astype(jnp.float32)
    mid = rest.astype(jnp.bfloat16)
    lo = (rest - mid.astype(jnp.float32)).astype(jnp.bfloat16)
    return [hi, mid, lo]


def nt(a, b):
    return lax.dot_general(a, b, (((1,), (1,)), ((), ())), preferred_element_type=jnp.float32)


def source_kernel(block, res_ref, cell_ref, off_ref, w_ref, tr_ref, out_ref, table, info):
    bx, by, bz = block
    starts = [lax.axis_index(a) * n for a, n in zip(AXES, block)]
    taps, mics = w_ref.shape
    steps = res_ref.shape[1]
    rel = [cell_ref[d : d + 1, :] - starts[d] for d in range(3)]
    near = functools.reduce(
        jnp.logical_and, [(rel[d] >= -4) & (rel[d] < block[d] + 4) for d in range(3)]
    )
    at = [rel[d] + off_ref[d] for d in range(3)]
    inside = functools.reduce(
        jnp.logical_and, [(at[d] >= 0) & (at[d] < block[d]) for d in range(3)]
    )
    row = jnp.where(inside, at[0] * by + at[1], -1)
    col = jnp.where(inside, at[2], -1)
    table[0:taps, :] = row.astype(jnp.float32).astype(jnp.bfloat16)
    table[taps : 2 * taps, :] = col.astype(jnp.float32).astype(jnp.bfloat16)
    for i, part in enumerate(split3(w_ref[...])):
        table[(2 + i) * taps : (3 + i) * taps, :] = part
    near_f = jnp.where(near, 1.0, 0.0)
    lanes = 128
    blocks = mics // lanes
    tri = (
        lax.broadcasted_iota(jnp.int32, (lanes, lanes), 0)
        < lax.broadcasted_iota(jnp.int32, (lanes, lanes), 1)
    )
    tri = jnp.where(tri, 1.0, 0.0).astype(jnp.bfloat16)
    base = jnp.float32(0.0)
    for i in range(blocks):
        part = near_f[:, i * lanes : (i + 1) * lanes]
        before = jnp.dot(
            jnp.broadcast_to(part, (8, lanes)).astype(jnp.bfloat16),
            tri,
            preferred_element_type=jnp.float32,
        )[0:1]
        slot = jnp.where(part > 0.5, before + base, -1.0)
        info[0:1, i * lanes : (i + 1) * lanes] = slot
        base = base + jnp.sum(part)
    count = base.astype(jnp.int32)
    out_ref[...] = jnp.zeros_like(out_ref)
    share = 2
    held = lanes // share
    per = taps // share
    part_of = lax.broadcasted_iota(jnp.int32, (per, lanes), 1) // held

    def spread(v):
        out = v[0:per]
        for i in range(1, share):
            out = jnp.where(part_of == i, v[i * per : (i + 1) * per], out)
        return out

    def chunk(j, carry):
        slots = (lax.broadcasted_iota(jnp.int32, (lanes, mics), 0) % held + j * held).astype(jnp.float32)
        sel = jnp.where(slots == info[0:1, :], 1.0, 0.0)
        mic_id = lax.broadcasted_iota(jnp.int32, (1, mics), 1).astype(jnp.float32)
        mic = jnp.sum(sel * (mic_id + 1.0), axis=1, keepdims=True) - 1.0
        sel_r = jnp.where(tr_ref[...].astype(jnp.float32) == mic, 1.0, 0.0).astype(jnp.bfloat16)
        tab = nt(table[...], sel.astype(jnp.bfloat16))
        rows = spread(tab[0:taps])
        cols = spread(tab[taps : 2 * taps])
        weights = spread(
            tab[2 * taps : 3 * taps] + tab[3 * taps : 4 * taps] + tab[4 * taps : 5 * taps]
        )
        whole = jnp.concatenate([res_ref[g] for g in range(res_ref.shape[0])], axis=1)
        res = sum(nt(part, sel_r) for part in split3(whole))
        iota_row = lax.broadcasted_iota(jnp.int32, (bx * by, lanes), 0).astype(jnp.float32)
        iota_col = lax.broadcasted_iota(jnp.int32, (bz, lanes), 0).astype(jnp.float32)
        group = 4
        for t0 in range(0, per, group):
            left, right = [[] for _ in range(steps)], []
            for t in range(t0, t0 + group):
                row_hot = iota_row == rows[t : t + 1]
                col_hot = jnp.where(iota_col == cols[t : t + 1], 1.0, 0.0).astype(jnp.bfloat16)
                right += [col_hot, col_hot]
                for n in range(steps):
                    amount = weights[t : t + 1] * res[n : n + 1]
                    hi = amount.astype(jnp.bfloat16).astype(jnp.float32)
                    lo = amount - hi
                    left[n].append(jnp.where(row_hot, hi, 0.0).astype(jnp.bfloat16))
                    left[n].append(jnp.where(row_hot, lo, 0.0).astype(jnp.bfloat16))
            right = jnp.concatenate(right, axis=1)
            for n in range(steps):
                out_ref[n] += nt(jnp.concatenate(left[n], axis=1), right)
        return carry

    lax.fori_loop(0, (count + held - 1) // held, chunk, 0)


def build_sources(block, residual, receiver_cell, tap_offset, tap_weight, trace_receiver):
    steps = residual.shape[1]
    taps, mics = tap_weight.shape
    return pl.pallas_call(
        functools.partial(source_kernel, block),
        out_shape=jax.ShapeDtypeStruct((steps, block[0] * block[1], block[2]), jnp.float32),
        in_specs=[pl.BlockSpec(memory_space=pltpu.VMEM)] * 5,
        out_specs=pl.BlockSpec(memory_space=pltpu.VMEM),
        scratch_shapes=[
            pltpu.VMEM((5 * taps, mics), jnp.bfloat16),
            pltpu.VMEM((8, mics), jnp.float32),
        ],
        compiler_params=pltpu.CompilerParams(vmem_limit_bytes=40 * 2**20),
        name="sources",
    )(residual, receiver_cell, tap_offset, tap_weight, trace_receiver.reshape(1, mics))


def matrices(nx, ny, nz):
    weight = {k: round(5040 * C[abs(k)]) if k else 0 for k in range(-4, 5)}
    at = np.vectorize(lambda k: weight.get(int(k), 0))
    x, y = np.divmod(np.arange(nx * ny), ny)
    dx, dy = x[:, None] - x[None, :], y[:, None] - y[None, :]
    inner = at(dx) * (dy == 0) + at(dy) * (dx == 0)
    fx, fy = np.divmod(np.arange(4 * ny), ny)
    tile, sub = np.divmod(np.arange(4 * nx), 8)
    lo_x = tile + np.where(sub >= 4, 0, nx // 2)
    hi_x = tile + np.where(sub < 4, 0, nx // 2)
    face_x = np.concatenate([fx - 4, fx + nx, lo_x, hi_x])
    face_y = np.concatenate([fy, fy, sub % 4 - 4, sub % 4 + ny])
    dx, dy = x[:, None] - face_x[None, :], y[:, None] - face_y[None, :]
    faces = at(dx) * (dy == 0) + at(dy) * (dx == 0)
    z = np.arange(nz)
    along = at(z[:, None] - z[None, :])
    end = np.arange(128)
    end = np.where(end < 64, end + nz, end - 128)
    ends = at(end[:, None] - z[None, :])
    return [m.astype(ml_dtypes.bfloat16) for m in (inner, faces, along, ends)]


def nn(a, b):
    return jnp.dot(a, b, preferred_element_type=jnp.float32)


class Halo:
    def __init__(self, sizes, ny, shape, hl, zl, ys, send_sem, recv_sem):
        self.ny, (self.rows, self.nz) = ny, shape
        self.nx = self.rows // ny
        self.hl, self.zl, self.ys = hl, zl, ys
        self.send_sem, self.recv_sem = send_sem, recv_sem
        me = [lax.axis_index(a) for a in AXES]
        self.has, self.to = [], []
        for d in range(3):
            self.has += [me[d] > 0, me[d] < sizes[d] - 1]
            self.to += [
                {AXES[d]: jnp.maximum(me[d] - 1, 0)},
                {AXES[d]: jnp.minimum(me[d] + 1, sizes[d] - 1)},
            ]

    def landing(self, slot, f):
        edge = (4 * self.ny, 4 * self.ny, 4 * self.nx, 4 * self.nx)
        if f >= 4:
            return self.zl.at[slot, f - 4]
        return self.hl.at[slot, pl.ds(sum(edge[:f]), edge[f])]

    def copy(self, slot, f_ref, f):
        rows, face = self.rows, 4 * self.ny
        src = (
            f_ref.at[pl.ds(0, face)],
            f_ref.at[pl.ds(rows - face, face)],
            self.ys.at[slot, 0],
            self.ys.at[slot, 1],
            f_ref.at[pl.ds(0, rows), pl.ds(0, 128)],
            f_ref.at[pl.ds(0, rows), pl.ds(self.nz - 128, 128)],
        )[f]
        return pltpu.make_async_remote_copy(
            src_ref=src,
            dst_ref=self.landing(slot, f ^ 1),
            send_sem=self.send_sem.at[slot, f],
            recv_sem=self.recv_sem.at[slot, f ^ 1],
            device_id=self.to[f],
            device_id_type=MESH,
        )

    def send(self, slot, f_ref):
        sub = lax.broadcasted_iota(jnp.int32, (8, self.nz), 0)
        nx, ny, ys = self.nx, self.ny, self.ys

        def start(f):
            @pl.when(self.has[f])
            def _():
                self.copy(slot, f_ref, f).start()

        for f in (0, 1, 4, 5):
            start(f)
        for i in range(nx // 2):
            lo, far = i * ny, (i + nx // 2) * ny
            a, b = f_ref[lo : lo + 8], f_ref[far : far + 8]
            ys[slot, 0, 8 * i : 8 * i + 8] = jnp.where(sub < 4, a, pltpu.roll(b, 4, 0))
            a, b = f_ref[lo + ny - 8 : lo + ny], f_ref[far + ny - 8 : far + ny]
            ys[slot, 1, 8 * i : 8 * i + 8] = jnp.where(sub >= 4, a, pltpu.roll(b, 4, 0))
        for f in (2, 3):
            start(f)

    def land(self, slot, faces):
        for f in faces:
            @pl.when(self.has[f])
            def _(f=f):
                dst = self.landing(slot, f)
                pltpu.make_async_remote_copy(
                    src_ref=dst, dst_ref=dst,
                    send_sem=self.send_sem.at[slot, f], recv_sem=self.recv_sem.at[slot, f],
                    device_id=self.to[f], device_id_type=MESH,
                ).wait_recv()

    def clear(self, slots):
        for f in range(6):
            @pl.when(jnp.logical_not(self.has[f]))
            def _(f=f):
                for slot in range(slots):
                    dst = self.landing(slot, f)
                    dst[...] = jnp.zeros(dst.shape, jnp.float32)

    def drain(self, slot, f_ref):
        for f in range(6):
            @pl.when(self.has[f])
            def _(f=f):
                self.copy(slot, f_ref, f).wait_send()


def local(f_ref, out, mats):
    f = f_ref[...]
    acc = 0.0
    for part in split3(f):
        acc = acc + nn(mats[0][...], part) + nn(part, mats[2][...])
    out[...] = acc * (1.0 / 5040.0) + (3.0 * C[0]) * f


def finish(halo, slot, out, mats):
    halo.land(slot, range(6))
    acc = 0.0
    for part in split3(halo.hl[slot]):
        acc = acc + nn(mats[1][...], part)
    lane = lax.broadcasted_iota(jnp.int32, (halo.rows, 128), 1)
    for part in split3(jnp.where(lane < 64, halo.zl[slot, 1], halo.zl[slot, 0])):
        acc = acc + nn(part, mats[3][...])
    return out[...] + acc * (1.0 / 5040.0)


def load(mats_in, mats, sem):
    moves = [pltpu.make_async_copy(a, b, sem.at[i]) for i, (a, b) in enumerate(zip(mats_in, mats))]
    for move in moves:
        move.start()
    return moves


def greet(halo, extra=()):
    barrier = pltpu.get_barrier_semaphore()
    for f in range(4 if extra else 6):
        @pl.when(halo.has[f])
        def _(f=f):
            pl.semaphore_signal(barrier, inc=1, device_id=halo.to[f], device_id_type=MESH)
    for other in extra:
        pl.semaphore_signal(barrier, inc=1, device_id=other, device_id_type=MESH)
    count = sum(h.astype(jnp.int32) for h in halo.has[: 4 if extra else 6])
    pl.semaphore_wait(barrier, count + len(extra))


def first_kernel(
    sizes, ny, p0, p1, q5, q4, cf, res, *rest
):
    mats_in, (p2, p3, lap1, lap2, q3, res_all) = rest[:4], rest[4:10]
    mats, (fq, lq, gath, hl, zl, ys, send_sem, recv_sem, mat_sem, res_send, res_recv) = (
        rest[10:14], rest[14:],
    )
    moves = load(mats_in, mats, mat_sem)
    halo = Halo(sizes, ny, p0.shape, hl, zl, ys, send_sem, recv_sem)
    gz, n = lax.axis_index("gz"), sizes[2]
    ahead = [{"gz": lax.rem(gz + k, n)} for k in range(1, n)]
    greet(halo, ahead)

    res_moves = [
        pltpu.make_async_remote_copy(
            src_ref=res, dst_ref=gath.at[gz],
            send_sem=res_send.at[k], recv_sem=res_recv.at[k],
            device_id=ahead[k], device_id_type=MESH,
        )
        for k in range(n - 1)
    ]
    for move in res_moves:
        move.start()
    halo.send(0, p1)
    fq[...] = cf[...] * q4[...]
    halo.send(1, fq)
    gath[gz] = res[...]
    halo.clear(3)
    for move in moves:
        move.wait()
    local(p1, lap1, mats)
    local(fq, lq, mats)
    full = finish(halo, 0, lap1, mats)
    lap1[...] = full
    p2[...] = 2.0 * p1[...] - p0[...] + cf[...] * full
    halo.send(2, p2)
    local(p2, lap2, mats)
    q3[...] = 2.0 * q4[...] - q5[...] + finish(halo, 1, lq, mats)
    for k in range(n - 1):
        dst = gath.at[lax.rem(gz + n - 1 - k, n)]
        pltpu.make_async_remote_copy(
            src_ref=dst, dst_ref=dst,
            send_sem=res_send.at[k], recv_sem=res_recv.at[k],
            device_id=ahead[k], device_id_type=MESH,
        ).wait_recv()
    res_all[...] = gath[...]
    full = finish(halo, 2, lap2, mats)
    lap2[...] = full
    p3[...] = 2.0 * p2[...] - p1[...] + cf[...] * full
    halo.drain(0, p1)
    halo.drain(1, fq)
    halo.drain(2, p2)
    for move in res_moves:
        move.wait_send()


def last_kernel(sizes, ny, steps, q4, cf, q3_part, lap1, lap2, p2, p3, src, *rest):
    mats_in, (grad, one, zero) = rest[:4], rest[4:7]
    mats, (fp, fq, lap, lq, qb, hl, zl, ys, send_sem, recv_sem, mat_sem) = rest[7:11], rest[11:]
    moves = load(mats_in, mats, mat_sem)
    halo = Halo(sizes, ny, cf.shape, hl, zl, ys, send_sem, recv_sem)
    greet(halo)

    def p_at(n):
        return {2: p2, 3: p3}[n] if n < 4 else fp.at[n - 4]

    def lap_at(n):
        return {1: lap1, 2: lap2}[n] if n < 3 else lap.at[n - 3]

    forward = steps - 2
    qb[0] = q3_part[...] + src[steps - 1]
    fq[0] = cf[...] * qb[0]
    halo.send(forward, fq.at[0])
    halo.send(0, p3)
    halo.clear(forward + steps - 1)
    for move in moves:
        move.wait()
    local(fq.at[0], lq, mats)
    local(p3, lap.at[0], mats)
    for r in range(1, steps):
        slot = forward + r - 1
        full = finish(halo, slot, lq, mats)
        now = qb.at[r - 1]
        old = q4 if r == 1 else qb.at[r - 2]
        new = 2.0 * now[...] - old[...] + full + src[steps - 1 - r]
        if r + 1 < steps:
            qb[r] = new
            fq[r] = cf[...] * new
            halo.send(slot + 1, fq.at[r])
            local(fq.at[r], lq, mats)
        else:
            zero[...] = new
            one[...] = now[...]
        n = r + 2
        if n <= steps:
            full = finish(halo, n - 3, lap_at(n), mats)
            lap_at(n)[...] = full
            if n < steps:
                fp[n - 3] = 2.0 * p_at(n)[...] - p_at(n - 1)[...] + cf[...] * full
                halo.send(n - 2, fp.at[n - 3])
                local(fp.at[n - 3], lap_at(n + 1), mats)
        if r == steps - 2:
            total = q4[...] * lap_at(steps)[...]
            for m in range(1, steps):
                total = total + qb[m - 1] * lap_at(steps - m)[...]
            grad[...] = total
    for n in range(3, steps + 1):
        halo.drain(n - 3, p_at(n))
    for r in range(1, steps):
        halo.drain(forward + r - 1, fq.at[r - 1])


def shards(sizes, p0, p1, q5, q4, cf, residual, receiver_cell, tap_offset, tap_weight, trace_receiver):
    nx, ny, nz = p0.shape
    steps = residual.shape[0]
    rows = nx * ny
    f32 = jnp.float32
    vmem, anywhere = pl.BlockSpec(memory_space=pltpu.VMEM), pl.BlockSpec(memory_space=pl.ANY)
    p0, p1, q5, q4, cf = [a.reshape(rows, nz) for a in (p0, p1, q5, q4, cf)]
    mats = matrices(nx, ny, nz)
    field = jax.ShapeDtypeStruct((rows, nz), f32)
    mat_scratch = [pltpu.VMEM(m.shape, jnp.bfloat16) for m in mats]

    def halo_scratch(slots):
        return [
            pltpu.VMEM((slots, 8 * (nx + ny), nz), f32),
            pltpu.VMEM((slots, 2, rows, 128), f32),
            pltpu.VMEM((slots, 2, 4 * nx, nz), f32),
            pltpu.SemaphoreType.DMA((slots, 6)),
            pltpu.SemaphoreType.DMA((slots, 6)),
            pltpu.SemaphoreType.DMA((4,)),
        ]

    gath = (sizes[2],) + residual.shape
    p2, p3, lap1, lap2, q3, res_all = pl.pallas_call(
        functools.partial(first_kernel, sizes, ny),
        out_shape=[field] * 5 + [jax.ShapeDtypeStruct(gath, f32)],
        in_specs=[vmem] * 6 + [anywhere] * 4,
        out_specs=[vmem] * 6,
        scratch_shapes=mat_scratch
        + [pltpu.VMEM((rows, nz), f32), pltpu.VMEM((rows, nz), f32), pltpu.VMEM(gath, f32)]
        + halo_scratch(3)
        + [pltpu.SemaphoreType.DMA((sizes[2],)), pltpu.SemaphoreType.DMA((sizes[2],))],
        compiler_params=pltpu.CompilerParams(
            collective_id=0, has_side_effects=True, vmem_limit_bytes=28 * 2**20
        ),
        name="first",
    )(p0, p1, q5, q4, cf, residual, *mats)
    src = build_sources((nx, ny, nz), res_all, receiver_cell, tap_offset, tap_weight, trace_receiver)
    outs = pl.pallas_call(
        functools.partial(last_kernel, sizes, ny, steps),
        out_shape=[field] * 3,
        in_specs=[vmem] * 8 + [anywhere] * 4,
        out_specs=[vmem] * 3,
        scratch_shapes=mat_scratch
        + [
            pltpu.VMEM((steps - 3, rows, nz), f32),
            pltpu.VMEM((steps - 1, rows, nz), f32),
            pltpu.VMEM((steps - 2, rows, nz), f32),
            pltpu.VMEM((rows, nz), f32),
            pltpu.VMEM((steps - 1, rows, nz), f32),
        ]
        + halo_scratch(2 * steps - 3),
        compiler_params=pltpu.CompilerParams(
            collective_id=1, has_side_effects=True, vmem_limit_bytes=40 * 2**20
        ),
        name="last",
    )(q4, cf, q3, lap1, lap2, p2, p3, src, *mats)
    return tuple(o.reshape(nx, ny, nz) for o in outs)


def solution(mesh):
    field = P(*AXES)
    return jax.shard_map(
        functools.partial(shards, tuple(mesh.shape[a] for a in AXES)),
        mesh=mesh,
        in_specs=(field,) * 5 + (P(None, "gz"), P(), P(), P(), P()),
        out_specs=(field,) * 3,
        check_vma=False,
    )
```

```python
import functools

import jax
import jax.numpy as jnp
from jax import lax
from jax.experimental import pallas as pl
from jax.experimental.pallas import tpu as pltpu
from jax.sharding import PartitionSpec as P

C = (-205.0 / 72.0, 8.0 / 5.0, -1.0 / 5.0, 8.0 / 315.0, -1.0 / 560.0)
AXES = ("gx", "gy", "gz")
MESH = pl.DeviceIdType.MESH


def split3(v):
    hi = v.astype(jnp.bfloat16)
    rest = v - hi.astype(jnp.float32)
    mid = rest.astype(jnp.bfloat16)
    lo = (rest - mid.astype(jnp.float32)).astype(jnp.bfloat16)
    return [hi, mid, lo]


def nt(a, b):
    return lax.dot_general(a, b, (((1,), (1,)), ((), ())), preferred_element_type=jnp.float32)


def source_kernel(block, res_ref, cell_ref, off_ref, w_ref, tr_ref, out_ref, table, info):
    bx, by, bz = block
    starts = [lax.axis_index(a) * n for a, n in zip(AXES, block)]
    taps, mics = w_ref.shape
    steps = res_ref.shape[1]
    rel = [cell_ref[d : d + 1, :] - starts[d] for d in range(3)]
    near = functools.reduce(
        jnp.logical_and, [(rel[d] >= -4) & (rel[d] < block[d] + 4) for d in range(3)]
    )
    at = [rel[d] + off_ref[d] for d in range(3)]
    inside = functools.reduce(
        jnp.logical_and, [(at[d] >= 0) & (at[d] < block[d]) for d in range(3)]
    )
    row = jnp.where(inside, at[0] * by + at[1], -1)
    col = jnp.where(inside, at[2], -1)
    table[0:taps, :] = row.astype(jnp.float32).astype(jnp.bfloat16)
    table[taps : 2 * taps, :] = col.astype(jnp.float32).astype(jnp.bfloat16)
    for i, part in enumerate(split3(w_ref[...])):
        table[(2 + i) * taps : (3 + i) * taps, :] = part
    near_f = jnp.where(near, 1.0, 0.0)
    lanes = 128
    blocks = mics // lanes
    tri = (
        lax.broadcasted_iota(jnp.int32, (lanes, lanes), 0)
        < lax.broadcasted_iota(jnp.int32, (lanes, lanes), 1)
    )
    tri = jnp.where(tri, 1.0, 0.0).astype(jnp.bfloat16)
    base = jnp.float32(0.0)
    for i in range(blocks):
        part = near_f[:, i * lanes : (i + 1) * lanes]
        before = jnp.dot(
            jnp.broadcast_to(part, (8, lanes)).astype(jnp.bfloat16),
            tri,
            preferred_element_type=jnp.float32,
        )[0:1]
        slot = jnp.where(part > 0.5, before + base, -1.0)
        info[0:1, i * lanes : (i + 1) * lanes] = slot
        base = base + jnp.sum(part)
    count = base.astype(jnp.int32)
    out_ref[...] = jnp.zeros_like(out_ref)
    share = 2
    held = lanes // share
    per = taps // share
    part_of = lax.broadcasted_iota(jnp.int32, (per, lanes), 1) // held

    def spread(v):
        out = v[0:per]
        for i in range(1, share):
            out = jnp.where(part_of == i, v[i * per : (i + 1) * per], out)
        return out

    def chunk(j, carry):
        slots = (lax.broadcasted_iota(jnp.int32, (lanes, mics), 0) % held + j * held).astype(jnp.float32)
        sel = jnp.where(slots == info[0:1, :], 1.0, 0.0)
        mic_id = lax.broadcasted_iota(jnp.int32, (1, mics), 1).astype(jnp.float32)
        mic = jnp.sum(sel * (mic_id + 1.0), axis=1, keepdims=True) - 1.0
        sel_r = jnp.where(tr_ref[...].astype(jnp.float32) == mic, 1.0, 0.0).astype(jnp.bfloat16)
        tab = nt(table[...], sel.astype(jnp.bfloat16))
        rows = spread(tab[0:taps])
        cols = spread(tab[taps : 2 * taps])
        weights = spread(
            tab[2 * taps : 3 * taps] + tab[3 * taps : 4 * taps] + tab[4 * taps : 5 * taps]
        )
        whole = jnp.concatenate([res_ref[g] for g in range(res_ref.shape[0])], axis=1)
        res = sum(nt(part, sel_r) for part in split3(whole))
        iota_row = lax.broadcasted_iota(jnp.int32, (bx * by, lanes), 0).astype(jnp.float32)
        iota_col = lax.broadcasted_iota(jnp.int32, (bz, lanes), 0).astype(jnp.float32)
        group = 4
        for t0 in range(0, per, group):
            left, right = [[] for _ in range(steps)], []
            for t in range(t0, t0 + group):
                row_hot = iota_row == rows[t : t + 1]
                col_hot = jnp.where(iota_col == cols[t : t + 1], 1.0, 0.0).astype(jnp.bfloat16)
                right += [col_hot, col_hot]
                for n in range(steps):
                    amount = weights[t : t + 1] * res[n : n + 1]
                    hi = amount.astype(jnp.bfloat16).astype(jnp.float32)
                    lo = amount - hi
                    left[n].append(jnp.where(row_hot, hi, 0.0).astype(jnp.bfloat16))
                    left[n].append(jnp.where(row_hot, lo, 0.0).astype(jnp.bfloat16))
            right = jnp.concatenate(right, axis=1)
            for n in range(steps):
                out_ref[n] += nt(jnp.concatenate(left[n], axis=1), right)
        return carry

    lax.fori_loop(0, (count + held - 1) // held, chunk, 0)


def build_sources(block, residual, receiver_cell, tap_offset, tap_weight, trace_receiver):
    steps = residual.shape[1]
    taps, mics = tap_weight.shape
    return pl.pallas_call(
        functools.partial(source_kernel, block),
        out_shape=jax.ShapeDtypeStruct((steps, block[0] * block[1], block[2]), jnp.float32),
        in_specs=[pl.BlockSpec(memory_space=pltpu.VMEM)] * 5,
        out_specs=pl.BlockSpec(memory_space=pltpu.VMEM),
        scratch_shapes=[
            pltpu.VMEM((5 * taps, mics), jnp.bfloat16),
            pltpu.VMEM((8, mics), jnp.float32),
        ],
        compiler_params=pltpu.CompilerParams(vmem_limit_bytes=32 * 2**20),
        name="sources",
    )(residual, receiver_cell, tap_offset, tap_weight, trace_receiver.reshape(1, mics))


def stencil(d):
    d = jnp.abs(d)
    return sum(jnp.where(d == k, float(round(5040 * C[k])), 0.0) for k in range(1, 5))


def cross(dx, dy):
    return jnp.where(dy == 0, stencil(dx), 0.0) + jnp.where(dx == 0, stencil(dy), 0.0)


def matrices(nx, ny, m_in, m_face, m_z, m_end):
    def grid(ref):
        return [lax.broadcasted_iota(jnp.int32, ref.shape, d) for d in range(2)]

    to, at = grid(m_in)
    m_in[...] = cross(to // ny - at // ny, to % ny - at % ny).astype(jnp.bfloat16)
    to, at = grid(m_face)
    x, y = to // ny, to % ny
    upper = at >= 4 * ny
    face = at - jnp.where(upper, 4 * ny, 0)
    in_x = cross(x - (face // ny + jnp.where(upper, nx, -4)), y - face % ny)
    pack = at - 8 * ny
    upper = pack >= 4 * nx
    pack = pack - jnp.where(upper, 4 * nx, 0)
    far = jnp.where(pack % 8 < 4, 0, 1) == jnp.where(upper, 1, 0)
    face_x = pack // 8 + jnp.where(far, nx // 2, 0)
    in_y = cross(x - face_x, y - (pack % 4 + jnp.where(upper, ny, -4)))
    m_face[...] = jnp.where(at < 8 * ny, in_x, in_y).astype(jnp.bfloat16)
    at, to = grid(m_z)
    m_z[...] = stencil(to - at).astype(jnp.bfloat16)
    at, to = grid(m_end)
    m_end[...] = stencil(to - jnp.where(at < 64, at + m_z.shape[0], at - 128)).astype(jnp.bfloat16)


def gather_kernel(n, block, res, out, m_in, m_face, m_z, m_end, land, send_sem, recv_sem):
    gz = lax.axis_index("gz")
    ahead = [{"gz": lax.rem(gz + k, n)} for k in range(1, n)]
    barrier = pltpu.get_barrier_semaphore()
    for other in ahead:
        pl.semaphore_signal(barrier, inc=1, device_id=other, device_id_type=MESH)
    pl.semaphore_wait(barrier, n - 1)
    moves = [
        pltpu.make_async_remote_copy(
            src_ref=res, dst_ref=land.at[gz],
            send_sem=send_sem.at[k], recv_sem=recv_sem.at[k],
            device_id=ahead[k], device_id_type=MESH,
        )
        for k in range(n - 1)
    ]
    for move in moves:
        move.start()
    matrices(block[0], block[1], m_in, m_face, m_z, m_end)
    land[gz] = res[...]
    for k in range(n - 1):
        dst = land.at[lax.rem(gz + n - 1 - k, n)]
        pltpu.make_async_remote_copy(
            src_ref=dst, dst_ref=dst,
            send_sem=send_sem.at[k], recv_sem=recv_sem.at[k],
            device_id=ahead[k], device_id_type=MESH,
        ).wait_recv()
    out[...] = land[...]
    for move in moves:
        move.wait_send()


def gather(sizes, block, residual):
    nx, ny, nz = block
    n = sizes[2]
    vmem = pl.BlockSpec(memory_space=pltpu.VMEM)
    shape = (n,) + residual.shape
    mats = [(nx * ny, nx * ny), (nx * ny, 8 * (nx + ny)), (nz, nz), (128, nz)]
    return pl.pallas_call(
        functools.partial(gather_kernel, n, block),
        out_shape=[jax.ShapeDtypeStruct(shape, jnp.float32)]
        + [jax.ShapeDtypeStruct(m, jnp.bfloat16) for m in mats],
        in_specs=[vmem],
        out_specs=[vmem] * 5,
        scratch_shapes=[
            pltpu.VMEM(shape, jnp.float32),
            pltpu.SemaphoreType.DMA((n,)),
            pltpu.SemaphoreType.DMA((n,)),
        ],
        compiler_params=pltpu.CompilerParams(
            collective_id=1, has_side_effects=True, vmem_limit_bytes=16 * 2**20
        ),
        cost_estimate=pl.CostEstimate(flops=4 * 10**9, bytes_accessed=12 * 10**6, transcendentals=0),
        name="gather",
    )(residual)


def nn(a, b):
    return jnp.dot(a, b, preferred_element_type=jnp.float32)


def wave_kernel(
    sizes, ny, p0, p1, q5, q4, cf, src, m_in, m_face, m_z, m_end, grad, one, zero,
    fp, fq, lap, lq, qb, hl, zl, ys, send_sem, recv_sem,
):
    steps = src.shape[0]
    rows, nz = p0.shape
    nx = rows // ny
    faces_rows = (4 * ny, 4 * ny, 4 * nx, 4 * nx)
    me = [lax.axis_index(a) for a in AXES]
    has = []
    for d in range(3):
        has += [me[d] > 0, me[d] < sizes[d] - 1]
    to = []
    for d in range(3):
        to += [{AXES[d]: jnp.maximum(me[d] - 1, 0)}, {AXES[d]: jnp.minimum(me[d] + 1, sizes[d] - 1)}]

    barrier = pltpu.get_barrier_semaphore()
    for f in range(6):
        @pl.when(has[f])
        def _(f=f):
            pl.semaphore_signal(barrier, inc=1, device_id=to[f], device_id_type=MESH)
    pl.semaphore_wait(barrier, sum(h.astype(jnp.int32) for h in has))

    sub = lax.broadcasted_iota(jnp.int32, (8, nz), 0)
    lane = lax.broadcasted_iota(jnp.int32, (rows, 128), 1)

    def field(ch, r):
        if r == 0 and ch == 0:
            return p1
        return (fp, fq)[ch].at[r]

    def landing(ch, r, f):
        if f >= 4:
            return zl.at[ch, r, f - 4]
        return hl.at[ch, r, pl.ds(sum(faces_rows[:f]), faces_rows[f])]

    def copies(ch, r):
        f_ref = field(ch, r)
        srcs = [
            f_ref.at[pl.ds(0, 4 * ny)],
            f_ref.at[pl.ds(rows - 4 * ny, 4 * ny)],
            ys.at[ch, r, 0],
            ys.at[ch, r, 1],
            f_ref.at[pl.ds(0, rows), pl.ds(0, 128)],
            f_ref.at[pl.ds(0, rows), pl.ds(nz - 128, 128)],
        ]
        return [
            pltpu.make_async_remote_copy(
                src_ref=srcs[f],
                dst_ref=landing(ch, r, f ^ 1),
                send_sem=send_sem.at[ch, r, f],
                recv_sem=recv_sem.at[ch, r, f ^ 1],
                device_id=to[f],
                device_id_type=MESH,
            )
            for f in range(6)
        ]

    def send(ch, r):
        f_ref = field(ch, r)
        moves = copies(ch, r)
        for f in (0, 1, 4, 5):
            @pl.when(has[f])
            def _(f=f):
                moves[f].start()
        for i in range(nx // 2):
            lo, far = i * ny, (i + nx // 2) * ny
            a, b = f_ref[lo : lo + 8], f_ref[far : far + 8]
            ys[ch, r, 0, 8 * i : 8 * i + 8] = jnp.where(sub < 4, a, pltpu.roll(b, 4, 0))
            a, b = f_ref[lo + ny - 8 : lo + ny], f_ref[far + ny - 8 : far + ny]
            ys[ch, r, 1, 8 * i : 8 * i + 8] = jnp.where(sub >= 4, a, pltpu.roll(b, 4, 0))
        for f in (2, 3):
            @pl.when(has[f])
            def _(f=f):
                moves[f].start()

    def land(ch, r):
        for f in range(6):
            @pl.when(has[f])
            def _(f=f):
                dst = landing(ch, r, f)
                pltpu.make_async_remote_copy(
                    src_ref=dst, dst_ref=dst,
                    send_sem=send_sem.at[ch, r, f], recv_sem=recv_sem.at[ch, r, f],
                    device_id=to[f], device_id_type=MESH,
                ).wait_recv()

    def local(ch, r, out):
        f = field(ch, r)[...]
        acc = 0.0
        for part in split3(f):
            acc = acc + nn(m_in[...], part) + nn(part, m_z[...])
        out[...] = acc * (1.0 / 5040.0) + (3.0 * C[0]) * f

    def finish(ch, r, out):
        land(ch, r)
        acc = 0.0
        for part in split3(hl[ch, r]):
            acc = acc + nn(m_face[...], part)
        for part in split3(jnp.where(lane < 64, zl[ch, r, 1], zl[ch, r, 0])):
            acc = acc + nn(part, m_end[...])
        return out[...] + acc * (1.0 / 5040.0)

    send(0, 0)
    fq[0] = cf[...] * q4[...]
    send(1, 0)
    for f in range(6):
        @pl.when(jnp.logical_not(has[f]))
        def _(f=f):
            for ch in range(2):
                for r in range(steps):
                    dst = landing(ch, r, f)
                    dst[...] = jnp.zeros(dst.shape, jnp.float32)

    local(0, 0, lap.at[0])
    local(1, 0, lq)
    for r in range(steps):
        full = finish(0, r, lap.at[r])
        lap[r] = full
        if r + 1 < steps:
            old = p0 if r == 0 else field(0, r - 1)
            fp[r + 1] = 2.0 * field(0, r)[...] - old[...] + cf[...] * full
            send(0, r + 1)
            local(0, r + 1, lap.at[r + 1])

        full = finish(1, r, lq)
        now = q4 if r == 0 else qb.at[r - 1]
        old = q5 if r == 0 else (q4 if r == 1 else qb.at[r - 2])
        new = 2.0 * now[...] - old[...] + full + src[steps - 1 - r]
        if r + 1 < steps:
            qb[r] = new
            fq[r + 1] = cf[...] * new
            send(1, r + 1)
            local(1, r + 1, lq)
        else:
            zero[...] = new
            one[...] = now[...]
            total = q4[...] * lap[steps - 1]
            for n in range(1, steps):
                total = total + qb[n - 1] * lap[steps - 1 - n]
            grad[...] = total

    for ch in range(2):
        for r in range(steps):
            moves = copies(ch, r)
            for f in range(6):
                @pl.when(has[f])
                def _(f=f):
                    moves[f].wait_send()


def wave(sizes, p0, p1, q5, q4, cf, src, mats):
    nx, ny, nz = p0.shape
    steps = src.shape[0]
    rows = nx * ny
    f32 = jnp.float32
    flat = [a.reshape(rows, nz) for a in (p0, p1, q5, q4, cf)]
    outs = pl.pallas_call(
        functools.partial(wave_kernel, sizes, ny),
        out_shape=[jax.ShapeDtypeStruct((rows, nz), f32)] * 3,
        in_specs=[pl.BlockSpec(memory_space=pltpu.VMEM)] * 10,
        out_specs=[pl.BlockSpec(memory_space=pltpu.VMEM)] * 3,
        scratch_shapes=[
            pltpu.VMEM((steps, rows, nz), f32),
            pltpu.VMEM((steps, rows, nz), f32),
            pltpu.VMEM((steps, rows, nz), f32),
            pltpu.VMEM((rows, nz), f32),
            pltpu.VMEM((steps, rows, nz), f32),
            pltpu.VMEM((2, steps, 8 * (nx + ny), nz), f32),
            pltpu.VMEM((2, steps, 2, rows, 128), f32),
            pltpu.VMEM((2, steps, 2, 4 * nx, nz), f32),
            pltpu.SemaphoreType.DMA((2, steps, 6)),
            pltpu.SemaphoreType.DMA((2, steps, 6)),
        ],
        compiler_params=pltpu.CompilerParams(
            collective_id=0, has_side_effects=True, vmem_limit_bytes=32 * 2**20
        ),
        name="wave",
    )(*flat, src, *mats)
    return [o.reshape(nx, ny, nz) for o in outs]


def shards(sizes, p0, p1, q5, q4, cf, residual, receiver_cell, tap_offset, tap_weight, trace_receiver):
    gathered, *mats = gather(sizes, p0.shape, residual)
    src = build_sources(p0.shape, gathered, receiver_cell, tap_offset, tap_weight, trace_receiver)
    return tuple(wave(sizes, p0, p1, q5, q4, cf, src, mats))


def solution(mesh):
    field = P(*AXES)
    return jax.shard_map(
        functools.partial(shards, tuple(mesh.shape[a] for a in AXES)),
        mesh=mesh,
        in_specs=(field,) * 5 + (P(None, "gz"), P(), P(), P(), P()),
        out_specs=(field,) * 3,
        check_vma=False,
    )
```
